32 devices in a mesh: tensor: 4 (over z), shard: 2 (over y), replica: 4 (over x, core).
Axes of the slice: x: 2, y: 2, z: 4, core: 2. Of those that a mesh axis runs over, the one named last changes fastest.
Arguments:
- block_in: float32 [8, 640, 1024], P(('shard', 'replica'), 'tensor'), may hold values from -12 to 12
- segment_ids: int32 [8, 640], P(('shard', 'replica')), may hold values from 0 to 3, never falling along the last dimension, each value on 1 to 256 neighbouring positions
- grad_out: float32 [8, 640, 1024], P(('shard', 'replica'), 'tensor'), may hold values from -6 to 6
- qkv_weight: bfloat16 [1024, 3, 1024], P('shard', None, 'tensor'), may hold values from -2 to 2
- qv_bias: bfloat16 [2, 1024], P(None, ('tensor', 'shard')), may hold values from -3 to 3
- out_weight: bfloat16 [1024, 1024], P('tensor', 'shard'), may hold values from -0.75 to 0.75
- up_weight: bfloat16 [1024, 4096], P('shard', 'tensor'), may hold values from -0.1875 to 0.1875
- up_bias: bfloat16 [4096], P(('tensor', 'shard')), may hold values from -3 to 3
- down_weight: bfloat16 [4096, 1024], P('tensor', 'shard'), may hold values from -0.09375 to 0.09375
- norm_gains: bfloat16 [2, 1024], P(None, 'shard'), may hold values from 0.25 to 1.75
- shift_biases: bfloat16 [4, 1024], P(None, 'shard'), may hold values from -3 to 3
Outputs:
- block_out: float32 [8, 640, 1024], P(('shard', 'replica'), 'tensor')
- grad_in: float32 [8, 640, 1024], P(('shard', 'replica'), 'tensor')
- grad_qkv_weight: float32 [1024, 3, 1024], P('shard', None, 'tensor')
- grad_qv_bias: float32 [2, 1024], P(None, ('tensor', 'shard'))
- grad_out_weight: float32 [1024, 1024], P('tensor', 'shard')
- grad_up_weight: float32 [1024, 4096], P('shard', 'tensor')
- grad_up_bias: float32 [4096], P(('tensor', 'shard'))
- grad_down_weight: float32 [4096, 1024], P('tensor', 'shard')
- grad_norm_gains: float32 [2, 1024], P(None, 'shard')
- grad_shift_biases: float32 [4, 1024], P(None, 'shard')
The draws below stay inside these ranges and needn't reach their ends.
Inputs may be any that keep to these rules, and one draw needn't show every extreme that they name: segment_ids never fall along a sequence; a document has 1 to 256 tokens, and one has exactly 256.
All inputs are finite; a program needn't handle non-finite values.
Results may differ from the reference program's by a relative error of at most 0.009.
The reference program's roundings to bfloat16 on the way count: a program that leaves them out, or rounds other values in their place, can miss the bound.
Values may be sent and summed in bfloat16 or wider, within the bound.
A program may use at most 128 MiB of HBM per device.

```python
import math
import jax
import jax.numpy as jnp
import numpy as np
from jax import lax

HEADS = 16
HEAD_DIM = 64
D = 1024
FF = 4096
SEQ_LEN = 640
DOCS = 4
SEG_MOST = 256
SEQS = 8


def draw_block_in(key, part):
    values = jax.random.normal(jax.random.fold_in(key, 11), (SEQS, SEQ_LEN, D), jnp.float32)
    return jnp.clip(values, -12.0, 12.0)


def draw_qkv_weight(key, part):
    values = jax.random.normal(jax.random.fold_in(key, 21), (D, 3, D), jnp.float32) * (1.0 / math.sqrt(D))
    return jnp.clip(values, -2.0, 2.0).astype(jnp.bfloat16)


def steps_of(stream_key, extent, pieces, least, largest):
    loudness = 1.0
    for dim, parts in pieces:
        heights = jax.random.uniform(jax.random.fold_in(jax.random.fold_in(stream_key, 6), dim), (parts,), jnp.float32, least / len(pieces), largest / len(pieces))
        loudness = loudness * jnp.repeat(jnp.exp(heights), extent[dim] // parts).reshape((-1,) + (1,) * (len(extent) - 1 - dim))
    return loudness


def length_profile(count, total, most, skew):
    weights = [(1 << 20) // math.isqrt(rank ** skew) + 1 for rank in range(2, count + 1)]
    spare, given = total - most - (count - 1), [1] * (count - 1)
    while spare > 0:
        candidates = [i for i in range(count - 1) if given[i] < most]
        whole, budget = sum([weights[i] for i in candidates]), spare
        for i in candidates:
            addition = min(most - given[i], max(1, budget * weights[i] // whole), spare)
            given[i] = given[i] + addition
            spare = spare - addition
    return np.array([most] + given)


def ragged(key, number_of, total, most, skew):
    if number_of == 2:
        one = jax.random.randint(key, (), max(1, total - most), min(most, total - 1) + 1)
        return jnp.stack([one, total - one])
    sizes = jnp.asarray(length_profile(number_of, total, most, skew), jnp.int32)
    twos = (number_of - 1) // 2
    giver, receiver = sizes[1:1 + 2 * twos:2], sizes[2:2 + 2 * twos:2]
    room = jnp.minimum(giver - 1, most - receiver)
    shifted = jax.random.randint(jax.random.fold_in(key, 1), (twos,), 0, 1 << 20) % (room + 1)
    sizes = sizes.at[1:1 + 2 * twos:2].set(giver - shifted).at[2:2 + 2 * twos:2].set(receiver + shifted)
    return sizes[jax.random.permutation(jax.random.fold_in(key, 2), number_of)]


def bell_draw(stream_key, shape, scale, most, shards=(), held_as=jnp.bfloat16):
    drawn = jax.random.normal(stream_key, shape, jnp.float32) * scale
    if len(shards) > 0:
        drawn = steps_of(stream_key, shape, shards, -0.22, 0.18) * drawn
    return jnp.clip(drawn, min=-most, max=most).astype(held_as)


def setup_inputs(seed: int = 0) -> dict:
    key_list = jax.random.split(jax.random.key(seed), 12)
    block_in = draw_block_in(jax.random.fold_in(key_list[11], 71), 0)
    segment_ids = jax.vmap(lambda own: jnp.searchsorted(jnp.cumsum(ragged(own, DOCS, SEQ_LEN, SEG_MOST, 2)), jnp.arange(SEQ_LEN), side="right"))(jax.random.split(key_list[1], SEQS)).reshape((SEQS, SEQ_LEN)).astype(jnp.int32)
    grad_out = bell_draw(key_list[2], (SEQS, SEQ_LEN, D), 1.0, 6.0, ((0, 8), (1, 4)), jnp.float32)
    qkv_weight = draw_qkv_weight(jax.random.fold_in(key_list[11], 71), 0)
    qv_bias = bell_draw(key_list[4], (2, D), 0.5, 3.0, ((1, 8),))
    out_weight = bell_draw(key_list[5], (D, D), (D // 16) ** -0.5, 0.75, ((0, 4), (1, 2)))
    up_weight = bell_draw(key_list[6], (D, FF), D ** -0.5, 0.1875, ((0, 2), (1, 4)))
    up_bias = bell_draw(key_list[7], (FF,), 0.5, 3.0, ((0, 8),))
    down_weight = bell_draw(key_list[8], (FF, D), FF ** -0.5, 0.09375, ((0, 4), (1, 2)))
    norm_gains = jnp.clip(1.0 + 0.15 * jax.random.normal(key_list[9], (2, D), jnp.float32), 0.25, 1.75).astype(jnp.bfloat16)
    shift_biases = bell_draw(key_list[10], (4, D), 0.5, 3.0, ((1, 2),))
    return dict(block_in=block_in, segment_ids=segment_ids, grad_out=grad_out, qkv_weight=qkv_weight, qv_bias=qv_bias, out_weight=out_weight, up_weight=up_weight, up_bias=up_bias, down_weight=down_weight, norm_gains=norm_gains, shift_biases=shift_biases)


norm_eps = 1e-12
masked_score = -1e+30
highest_prec = lax.Precision.HIGHEST

def product(left, right, form):
    return jnp.einsum(form, left.astype(jnp.float32), right.astype(jnp.float32), precision=highest_prec)

def norm_forward(summed, gain, shift):
    center = summed - lax.optimization_barrier(jnp.mean(summed, axis=-1, keepdims=True))
    inverse = lax.rsqrt(lax.optimization_barrier(jnp.mean(center * center, axis=-1, keepdims=True)) + norm_eps)
    normed = center * inverse
    return (normed * gain + shift, normed, inverse)

def norm_backward(grad, normed, inverse, gain):
    scaled = grad * gain
    return inverse * (scaled - lax.optimization_barrier(jnp.mean(scaled, axis=-1, keepdims=True)) - normed * lax.optimization_barrier(jnp.mean(scaled * normed, axis=-1, keepdims=True)))

def gelu_parts(pre_act):
    cumul = 0.5 * (1.0 + jax.scipy.special.erf(pre_act * 0.7071067811865476))
    density = jnp.exp(-0.5 * pre_act * pre_act) * 0.3989422804014327
    return (pre_act * cumul, cumul + pre_act * density)

def reference(block_in, segment_ids, grad_out, qkv_weight, qv_bias, out_weight, up_weight, up_bias, down_weight, norm_gains, shift_biases):
    scale = 1.0 / math.sqrt(HEAD_DIM)
    gain_full = norm_gains.astype(jnp.float32)
    shift_full = shift_biases.astype(jnp.float32)
    qv_full = qv_bias.astype(jnp.float32)
    upbias_full = up_bias.astype(jnp.float32)

    def one_sequence(carry, items):
        inputs, segs, grad_here = items
        inputs_bf = inputs.astype(jnp.bfloat16)
        query_key_value = product(inputs_bf, qkv_weight, 'ld,dce->lce')
        query = (query_key_value[:, 0] + qv_full[0]).astype(jnp.bfloat16).reshape(SEQ_LEN, HEADS, HEAD_DIM)
        keys = query_key_value[:, 1].astype(jnp.bfloat16).reshape(SEQ_LEN, HEADS, HEAD_DIM)
        values = (query_key_value[:, 2] + qv_full[1]).astype(jnp.bfloat16).reshape(SEQ_LEN, HEADS, HEAD_DIM)
        same = (segs[:, None] == segs[None, :])[None]
        scores = jnp.where(same, product(query, keys, 'qhe,khe->hqk') * scale, masked_score)
        highest = lax.optimization_barrier(jnp.max(scores, axis=-1, keepdims=True))
        expo = jnp.exp(scores - highest)
        total = lax.optimization_barrier(jnp.sum(expo, axis=-1, keepdims=True))
        probs = (expo / total).astype(jnp.bfloat16)
        log_total = highest + jnp.log(total)
        attention_context = product(probs, values, 'hqk,khe->qhe').astype(jnp.bfloat16).reshape(SEQ_LEN, D)
        first_sum = inputs + (product(attention_context, out_weight, 'le,ed->ld') + shift_full[0])
        hidden, normed_one, inverse_one = norm_forward(first_sum, gain_full[0], shift_full[1])
        hidden_bf = hidden.astype(jnp.bfloat16)
        pre_act = product(hidden_bf, up_weight, 'ld,df->lf') + upbias_full
        activ, slope = gelu_parts(pre_act)
        activation_bfloat = activ.astype(jnp.bfloat16)
        second_sum = hidden + (product(activation_bfloat, down_weight, 'lf,fd->ld') + shift_full[2])
        output, normed_two, inverse_two = norm_forward(second_sum, gain_full[1], shift_full[3])
        d_second = norm_backward(grad_here, normed_two, inverse_two, gain_full[1])
        d_second_bf = d_second.astype(jnp.bfloat16)
        down_weight_gradient = product(activation_bfloat, d_second_bf, 'lf,ld->fd')
        d_pre = product(d_second_bf, down_weight, 'ld,fd->lf') * slope
        g_upbias = lax.optimization_barrier(jnp.sum(d_pre, axis=0))
        preact_gradient_bfloat = d_pre.astype(jnp.bfloat16)
        up_weight_gradient = product(hidden_bf, preact_gradient_bfloat, 'ld,lf->df')
        d_hidden = product(preact_gradient_bfloat, up_weight, 'lf,df->ld') + d_second
        d_first = norm_backward(d_hidden, normed_one, inverse_one, gain_full[0])
        g_gains = jnp.stack([lax.optimization_barrier(jnp.sum(d_hidden * normed_one, axis=0)), lax.optimization_barrier(jnp.sum(grad_here * normed_two, axis=0))])
        g_shifts = jnp.stack([lax.optimization_barrier(jnp.sum(d_first, axis=0)), lax.optimization_barrier(jnp.sum(d_hidden, axis=0)), lax.optimization_barrier(jnp.sum(d_second, axis=0)), lax.optimization_barrier(jnp.sum(grad_here, axis=0))])
        d_first_bf = d_first.astype(jnp.bfloat16)
        output_weight_gradient = product(attention_context, d_first_bf, 'le,ld->ed')
        context_gradient = product(d_first_bf, out_weight, 'ld,ed->le').astype(jnp.bfloat16).reshape(SEQ_LEN, HEADS, HEAD_DIM)
        probs_back = jnp.exp(scores - log_total)
        d_probs = product(context_gradient, values, 'qhe,khe->hqk')
        row_dot = lax.optimization_barrier(jnp.sum(probs_back * d_probs, axis=-1, keepdims=True))
        d_scores = (probs_back * (d_probs - row_dot)).astype(jnp.bfloat16)
        d_query = product(d_scores, keys, 'hqk,khe->qhe') * scale
        d_keys = product(d_scores, query, 'hqk,qhe->khe') * scale
        d_values = product(probs_back.astype(jnp.bfloat16), context_gradient, 'hqk,qhe->khe')
        d_query = d_query.reshape(SEQ_LEN, D)
        d_keys = d_keys.reshape(SEQ_LEN, D)
        d_values = d_values.reshape(SEQ_LEN, D)
        g_qv = jnp.stack([lax.optimization_barrier(jnp.sum(d_query, axis=0)), lax.optimization_barrier(jnp.sum(d_values, axis=0))])
        projected_gradient_bfloat = jnp.stack([d_query, d_keys, d_values], axis=1).astype(jnp.bfloat16)
        projection_weight_gradient = product(inputs_bf, projected_gradient_bfloat, 'ld,lce->dce')
        grad_input = product(projected_gradient_bfloat, qkv_weight, 'lce,dce->ld') + d_first
        updates = (projection_weight_gradient, g_qv, output_weight_gradient, up_weight_gradient, g_upbias, down_weight_gradient, g_gains, g_shifts)
        carry = tuple((old + new for old, new in zip(carry, updates)))
        return (carry, (output, grad_input))
    start = (jnp.zeros((D, 3, D), jnp.float32), jnp.zeros((2, D), jnp.float32), jnp.zeros((D, D), jnp.float32), jnp.zeros((D, FF), jnp.float32), jnp.zeros((FF,), jnp.float32), jnp.zeros((FF, D), jnp.float32), jnp.zeros((2, D), jnp.float32), jnp.zeros((4, D), jnp.float32))
    totals, (outputs, grads_in) = lax.scan(one_sequence, start, (block_in, segment_ids, grad_out))
    return (outputs, grads_in, totals[0], totals[1], totals[2], totals[3], totals[4], totals[5], totals[6], totals[7])
```

```python
import math

import jax
import jax.numpy as jnp
from jax import lax
from jax.sharding import PartitionSpec as P

HEAD_DIM = 64


norm_eps = 1e-12
masked_score = -1e30


def norm_forward(summed, gain, shift):
    center = summed - jnp.mean(summed, axis=-1, keepdims=True)
    inverse = lax.rsqrt(jnp.mean(center * center, axis=-1, keepdims=True) + norm_eps)
    normed = center * inverse
    return (normed * gain + shift, normed, inverse)


def norm_backward(grad, normed, inverse, gain):
    scaled = grad * gain
    return inverse * (
        scaled
        - jnp.mean(scaled, axis=-1, keepdims=True)
        - normed * jnp.mean(scaled * normed, axis=-1, keepdims=True)
    )


def gelu_parts(pre_act):
    cumul = 0.5 * (1.0 + jax.scipy.special.erf(pre_act * 0.7071067811865476))
    density = jnp.exp(-0.5 * pre_act * pre_act) * 0.3989422804014327
    return (pre_act * cumul, cumul + pre_act * density)


def scatter_sum(part, axes, dim):
    return lax.psum_scatter(
        part.astype(jnp.bfloat16), axes, scatter_dimension=dim, tiled=True
    )


def shards(
    block_in,
    segment_ids,
    grad_out,
    qkv_weight,
    qv_bias,
    out_weight,
    up_weight,
    up_bias,
    down_weight,
    norm_gains,
    shift_biases,
):
    small = (qv_bias, up_bias[None], norm_gains, shift_biases)
    packed = lax.all_gather(
        jnp.concatenate([vec.reshape(-1) for vec in small]), "shard", axis=0
    )
    unpacked = []
    start = 0
    for vec in small:
        rows, piece = vec.shape
        part = packed[:, start : start + rows * piece].reshape(-1, rows, piece)
        unpacked.append(jnp.swapaxes(part, 0, 1).reshape(rows, -1))
        start += rows * piece
    qv_packed, upbias_packed, gain_packed, shift_packed = unpacked
    upbias_packed = upbias_packed[0]
    (
        query_key_value_full,
        qv_all,
        output_weight_full,
        up_weight_full,
        upbias_all,
        down_weight_full,
        gain_all,
        shift_all,
    ) = (
        lax.all_gather(qkv_weight, "shard", axis=0, tiled=True),
        qv_packed,
        lax.all_gather(out_weight, "shard", axis=1, tiled=True),
        lax.all_gather(up_weight, "shard", axis=0, tiled=True),
        upbias_packed,
        lax.all_gather(down_weight, "shard", axis=1, tiled=True),
        gain_packed,
        shift_packed,
    )
    seqs = block_in.shape[0]
    width = block_in.shape[2]
    length = segment_ids.shape[1]
    cols = query_key_value_full.shape[2]
    heads_here = cols // HEAD_DIM
    scale = 1.0 / math.sqrt(HEAD_DIM)
    gain_full = gain_all.astype(jnp.float32)
    shift_full = shift_all.astype(jnp.float32)
    qv_full = qv_all.astype(jnp.float32)
    inputs_bf = block_in.astype(jnp.bfloat16)
    input_rows_full = lax.all_gather(inputs_bf, "tensor", axis=1, tiled=True)
    query_key_value = jnp.einsum(
        "agp,pmy->agmy", input_rows_full, query_key_value_full, preferred_element_type=jnp.float32
    )
    query = (
        (query_key_value[:, :, 0] + qv_full[0])
        .astype(jnp.bfloat16)
        .reshape(seqs, length, heads_here, HEAD_DIM)
    )
    keys = query_key_value[:, :, 1].astype(jnp.bfloat16).reshape(seqs, length, heads_here, HEAD_DIM)
    values = (
        (query_key_value[:, :, 2] + qv_full[1])
        .astype(jnp.bfloat16)
        .reshape(seqs, length, heads_here, HEAD_DIM)
    )
    same = (segment_ids[:, :, None] == segment_ids[:, None, :])[:, None]
    scores = jnp.einsum("sqhe,skhe->shqk", query, keys, preferred_element_type=jnp.float32) * scale
    scores = jnp.where(same, scores, masked_score)
    highest = jnp.max(scores, axis=-1, keepdims=True)
    expo = jnp.exp(scores - highest)
    total = jnp.sum(expo, axis=-1, keepdims=True)
    probs = (expo / total).astype(jnp.bfloat16)
    log_total = highest + jnp.log(total)
    attention_context = jnp.einsum(
        "shqk,skhe->sqhe", probs, values, preferred_element_type=jnp.float32
    )
    attention_context = attention_context.astype(jnp.bfloat16).reshape(seqs, length, cols)
    attention_slice = jnp.einsum(
        "nip,pr->nir", attention_context, output_weight_full, preferred_element_type=jnp.float32
    )
    attended = scatter_sum(attention_slice, "tensor", 1).astype(jnp.float32)
    first_sum = block_in + (attended + shift_full[0])
    hidden, normed_one, inverse_one = norm_forward(first_sum, gain_full[0], shift_full[1])
    hidden_bf = hidden.astype(jnp.bfloat16)
    hidden_state_full = lax.all_gather(hidden_bf, "tensor", axis=1, tiled=True)
    pre_act = jnp.einsum(
        "peo,ot->pet", hidden_state_full, up_weight_full, preferred_element_type=jnp.float32
    ) + upbias_all.astype(jnp.float32)
    activ, slope = gelu_parts(pre_act)
    activation_bfloat = activ.astype(jnp.bfloat16)
    down_weight_slice = jnp.einsum(
        "uzt,tv->uzv", activation_bfloat, down_weight_full, preferred_element_type=jnp.float32
    )
    second_sum = hidden + (
        scatter_sum(down_weight_slice, "tensor", 1).astype(jnp.float32)
        + shift_full[2]
    )
    block_out, normed_two, inverse_two = norm_forward(second_sum, gain_full[1], shift_full[3])
    d_second = norm_backward(grad_out, normed_two, inverse_two, gain_full[1])
    second_gradient_full = lax.all_gather(
        d_second.astype(jnp.bfloat16), "tensor", axis=1, tiled=True
    )
    down_weight_gradient = jnp.einsum(
        "bct,bcm->tm", activation_bfloat, second_gradient_full, preferred_element_type=jnp.float32
    )
    d_pre = (
        jnp.einsum(
            "ajn,tn->ajt",
            second_gradient_full,
            down_weight_full,
            preferred_element_type=jnp.float32,
        )
        * slope
    )
    g_upbias = jnp.sum(d_pre, axis=(0, 1))
    preact_gradient_bfloat = d_pre.astype(jnp.bfloat16)
    up_weight_gradient = jnp.einsum(
        "ahk,ahp->kp", hidden_state_full, preact_gradient_bfloat, preferred_element_type=jnp.float32
    )
    hidden_state_slice = jnp.einsum(
        "ixj,gj->ixg", preact_gradient_bfloat, up_weight_full, preferred_element_type=jnp.float32
    )
    d_hidden = (
        scatter_sum(hidden_state_slice, "tensor", 1).astype(jnp.float32) + d_second
    )
    d_first = norm_backward(d_hidden, normed_one, inverse_one, gain_full[0])
    gain_part = jnp.stack(
        [jnp.sum(d_hidden * normed_one, axis=(0, 1)), jnp.sum(grad_out * normed_two, axis=(0, 1))]
    )
    shift_part = jnp.stack(
        [
            jnp.sum(d_first, axis=(0, 1)),
            jnp.sum(d_hidden, axis=(0, 1)),
            jnp.sum(d_second, axis=(0, 1)),
            jnp.sum(grad_out, axis=(0, 1)),
        ]
    )
    first_gradient_full = lax.all_gather(d_first.astype(jnp.bfloat16), "tensor", axis=1, tiled=True)
    output_weight_gradient = jnp.einsum(
        "unb,una->ba", attention_context, first_gradient_full, preferred_element_type=jnp.float32
    )
    context_gradient = jnp.einsum(
        "tbu,wu->tbw", first_gradient_full, output_weight_full, preferred_element_type=jnp.float32
    )
    context_gradient = context_gradient.astype(jnp.bfloat16).reshape(
        seqs, length, heads_here, HEAD_DIM
    )
    probs_back = jnp.exp(scores - log_total)
    d_probs = jnp.einsum(
        "sqhe,skhe->shqk", context_gradient, values, preferred_element_type=jnp.float32
    )
    row_dot = jnp.sum(probs_back * d_probs, axis=-1, keepdims=True)
    d_scores = (probs_back * (d_probs - row_dot)).astype(jnp.bfloat16)
    d_query = (
        jnp.einsum("shqk,skhe->sqhe", d_scores, keys, preferred_element_type=jnp.float32) * scale
    )
    d_keys = (
        jnp.einsum("shqk,sqhe->skhe", d_scores, query, preferred_element_type=jnp.float32) * scale
    )
    d_values = jnp.einsum(
        "shqk,sqhe->skhe",
        probs_back.astype(jnp.bfloat16),
        context_gradient,
        preferred_element_type=jnp.float32,
    )
    d_query = d_query.reshape(seqs, length, cols)
    d_keys = d_keys.reshape(seqs, length, cols)
    d_values = d_values.reshape(seqs, length, cols)
    g_qv = jnp.stack([jnp.sum(d_query, axis=(0, 1)), jnp.sum(d_values, axis=(0, 1))])
    projected_gradient_bfloat = jnp.stack([d_query, d_keys, d_values], axis=2).astype(jnp.bfloat16)
    projection_weight_gradient = jnp.einsum(
        "pjx,pjvy->xvy",
        input_rows_full,
        projected_gradient_bfloat,
        preferred_element_type=jnp.float32,
    )
    input_slice = jnp.einsum(
        "pxvk,yvk->pxy",
        projected_gradient_bfloat,
        query_key_value_full,
        preferred_element_type=jnp.float32,
    )
    grad_in = scatter_sum(input_slice, "tensor", 1).astype(jnp.float32) + d_first
    matrices = (
        projection_weight_gradient,
        output_weight_gradient,
        up_weight_gradient,
        down_weight_gradient,
    )
    spread = (
        scatter_sum(matrices[0], ("shard", "replica"), 0),
        scatter_sum(matrices[1], ("shard", "replica"), 1),
        scatter_sum(matrices[2], ("shard", "replica"), 0),
        scatter_sum(matrices[3], ("shard", "replica"), 1),
    )
    summed = (
        lax.all_gather(spread[0], "replica", axis=0, tiled=True).astype(jnp.float32),
        lax.all_gather(spread[1], "replica", axis=1, tiled=True).astype(jnp.float32),
        lax.all_gather(spread[2], "replica", axis=0, tiled=True).astype(jnp.float32),
        lax.all_gather(spread[3], "replica", axis=1, tiled=True).astype(jnp.float32),
    )
    tensor_index = lax.axis_index("tensor")
    shard_index = lax.axis_index("shard")
    shard_count = lax.axis_size("shard")
    tensor_count = lax.axis_size("tensor")
    upbias_width = upbias_all.shape[0]
    qv_wide = lax.dynamic_update_slice(
        jnp.zeros((2, width), jnp.float32), g_qv, (0, tensor_index * cols)
    )
    upbias_wide = lax.dynamic_update_slice(
        jnp.zeros((upbias_width * tensor_count,), jnp.float32),
        g_upbias,
        (tensor_index * upbias_width,),
    )
    gain_tot, shift_tot, qv_tot, upbias_tot = lax.psum(
        (gain_part, shift_part, qv_wide, upbias_wide), ("tensor", "shard", "replica")
    )
    vec_piece = norm_gains.shape[1]
    qv_piece = qv_bias.shape[1]
    upbias_piece = up_bias.shape[0]
    owner_index = tensor_index * shard_count + shard_index
    grad_gains = lax.dynamic_slice_in_dim(gain_tot, shard_index * vec_piece, vec_piece, 1)
    grad_shifts = lax.dynamic_slice_in_dim(shift_tot, shard_index * vec_piece, vec_piece, 1)
    grad_qv = lax.dynamic_slice_in_dim(qv_tot, owner_index * qv_piece, qv_piece, 1)
    grad_upbias = lax.dynamic_slice_in_dim(upbias_tot, owner_index * upbias_piece, upbias_piece, 0)
    return (
        block_out,
        grad_in,
        summed[0],
        grad_qv,
        summed[1],
        summed[2],
        grad_upbias,
        summed[3],
        grad_gains,
        grad_shifts,
    )


def solution(mesh):
    in_specs = (
        P(("shard", "replica"), "tensor", None),
        P(("shard", "replica"), None),
        P(("shard", "replica"), "tensor", None),
        P("shard", None, "tensor"),
        P(None, ("tensor", "shard")),
        P("tensor", "shard"),
        P("shard", "tensor"),
        P(("tensor", "shard")),
        P("tensor", "shard"),
        P(None, "shard"),
        P(None, "shard"),
    )
    out_specs = (
        P(("shard", "replica"), "tensor", None),
        P(("shard", "replica"), "tensor", None),
        P("shard", None, "tensor"),
        P(None, ("tensor", "shard")),
        P("tensor", "shard"),
        P("shard", "tensor"),
        P(("tensor", "shard")),
        P("tensor", "shard"),
        P(None, "shard"),
        P(None, "shard"),
    )
    return jax.shard_map(shards, mesh=mesh, in_specs=in_specs, out_specs=out_specs, check_vma=False)
```

```python
import functools
import math

import jax
import jax.numpy as jnp
from jax import lax
from jax.experimental import pallas as pl
from jax.experimental.pallas import tpu as pltpu
from jax.sharding import PartitionSpec as P

HEAD_DIM = 64


norm_eps = 1e-12
masked_score = -1e30


def norm_forward(summed, gain, shift):
    center = summed - jnp.mean(summed, axis=-1, keepdims=True)
    inverse = lax.rsqrt(jnp.mean(center * center, axis=-1, keepdims=True) + norm_eps)
    normed = center * inverse
    return (normed * gain + shift, normed, inverse)


def norm_backward(grad, normed, inverse, gain):
    scaled = grad * gain
    return inverse * (
        scaled
        - jnp.mean(scaled, axis=-1, keepdims=True)
        - normed * jnp.mean(scaled * normed, axis=-1, keepdims=True)
    )


def gelu_parts(pre_act):
    cumul = 0.5 * (1.0 + jax.scipy.special.erf(pre_act * 0.7071067811865476))
    density = jnp.exp(-0.5 * pre_act * pre_act) * 0.3989422804014327
    return (pre_act * cumul, cumul + pre_act * density)


def scatter_sum(part, axes, dim):
    return lax.psum_scatter(
        part.astype(jnp.bfloat16), axes, scatter_dimension=dim, tiled=True
    )


def remote(src, dst, send, recv, where):
    return pltpu.make_async_remote_copy(
        src_ref=src,
        dst_ref=dst,
        send_sem=send,
        recv_sem=recv,
        device_id=where,
        device_id_type=pl.DeviceIdType.MESH,
    )


def greet(peers):
    barrier = pltpu.get_barrier_semaphore()
    for where in peers:
        pl.semaphore_signal(
            barrier, inc=1, device_id=where, device_id_type=pl.DeviceIdType.MESH
        )
    pl.semaphore_wait(barrier, len(peers))


def block_of(ref, kind, shape, piece, half):
    rows, cols = shape
    depth = rows // 2
    if kind == 0:
        return ref.at[pl.ds(pl.multiple_of(piece * rows + half * depth, depth), depth), :]
    return ref.at[
        pl.ds(pl.multiple_of(half * depth, depth), depth),
        pl.ds(pl.multiple_of(piece * cols, cols), cols),
    ]


def gather_kernel(n, kinds, shapes, *refs):
    count = len(kinds)
    ins, outs = refs[:count], refs[count : 2 * count]
    local, far_send, far_recv, near_send, near_recv = refs[2 * count :]
    me = lax.axis_index("shard")
    rep = lax.axis_index("replica")
    core = lax.rem(rep, 2)
    partner = {"replica": rep + 1 - 2 * core}
    greet([{"shard": lax.rem(me + k, n)} for k in range(1, n)] + [partner])
    far, near = {}, {}
    for i in range(count):
        for k in range(1, n):
            where = {"shard": lax.rem(me + k, n)}
            if kinds[i] == 2:
                src, dst = ins[i], outs[i].at[me]
            else:
                depth = shapes[i][0] // 2
                src = ins[i].at[pl.ds(pl.multiple_of(core * depth, depth), depth), :]
                dst = block_of(outs[i], kinds[i], shapes[i], me, core)
            far[i, k] = remote(src, dst, far_send.at[i, k - 1], far_recv.at[i, k - 1], where)
            far[i, k].start()
    own = []
    for i in range(count):
        rows, cols = shapes[i]
        if kinds[i] == 2:
            dst = outs[i].at[me]
        elif kinds[i] == 0:
            dst = outs[i].at[pl.ds(pl.multiple_of(me * rows, rows), rows), :]
        else:
            dst = outs[i].at[:, pl.ds(pl.multiple_of(me * cols, cols), cols)]
        own.append(pltpu.make_async_copy(ins[i], dst, local.at[i]))
        own[-1].start()
    for i in range(count):
        for k in range(1, n):
            far[i, k].wait_recv()
            if kinds[i] != 2:
                block = block_of(outs[i], kinds[i], shapes[i], lax.rem(me + n - k, n), core)
                near[i, k] = remote(
                    block, block, near_send.at[i, k - 1], near_recv.at[i, k - 1], partner
                )
                near[i, k].start()
    for copy in near.values():
        copy.wait()
    for copy in far.values():
        copy.wait_send()
    for copy in own:
        copy.wait()


def gather_blocks(arrays, kinds, ident):
    n = lax.axis_size("shard")
    shapes = [a.shape for a in arrays]
    out = []
    for a, kind in zip(arrays, kinds):
        rows, cols = a.shape
        full = ((n * rows, cols), (rows, n * cols), (n, rows, cols))[kind]
        out.append(jax.ShapeDtypeStruct(full, a.dtype))
    vmem = pl.BlockSpec(memory_space=pltpu.VMEM)
    grid = (len(arrays), max(n - 1, 1))
    total = sum(a.size * a.dtype.itemsize for a in arrays) * n
    return pl.pallas_call(
        functools.partial(gather_kernel, n, kinds, shapes),
        out_shape=out,
        in_specs=[vmem] * len(arrays),
        out_specs=[vmem] * len(arrays),
        scratch_shapes=[pltpu.SemaphoreType.DMA((len(arrays),))]
        + [pltpu.SemaphoreType.DMA(grid)] * 4,
        cost_estimate=pl.CostEstimate(
            flops=0, bytes_accessed=20 * total, transcendentals=0
        ),
        compiler_params=pltpu.CompilerParams(collective_id=ident, has_side_effects=True),
    )(*arrays)


def row_loop(rows, body):
    step = min(rows, 32)

    @pl.loop(0, rows // step)
    def _(j):
        body(pl.ds(pl.multiple_of(j * step, step), step))


def grad_kernel(n, m, kinds, *refs):
    count = len(kinds)
    ins, outs = refs[:count], refs[count : 2 * count]
    got, half, pieces, slots = (refs[(2 + q) * count : (3 + q) * count] for q in range(4))
    a_send, a_recv, b_send, b_recv, c_send, c_recv, d_send, d_recv = refs[6 * count :]
    me = lax.axis_index("shard")
    rep = lax.axis_index("replica")
    core = lax.rem(rep, 2)
    chips = m // 2
    chip = rep // 2
    partner = {"replica": rep + 1 - 2 * core}
    shard_peers = [{"shard": lax.rem(me + k, n)} for k in range(1, n)]
    chip_peers = [{"replica": lax.rem(chip + k, chips) * 2 + core} for k in range(1, chips)]
    greet([partner] + shard_peers + chip_peers)
    f32 = jnp.float32
    first, second, third, fourth = [], {}, {}, []

    def piece_of(i, index):
        if kinds[i] == 0:
            return half[i].at[index]
        cols = outs[i].shape[2]
        return half[i].at[:, pl.ds(pl.multiple_of(index * cols, cols), cols)]

    for i in range(count):
        src = ins[i].at[:, 1 - core] if kinds[i] == 0 else ins[i].at[1 - core]
        first.append(remote(src, got[i], a_send.at[i], a_recv.at[i], partner))
        first[i].start()
    for i in range(count):
        first[i].wait_recv()
        rows = outs[i].shape[1]
        if kinds[i] == 0:

            @pl.loop(0, n)
            def _(p):
                def add(at):
                    half[i][p, at] = (
                        ins[i][p, core, at].astype(f32) + got[i][p, at].astype(f32)
                    ).astype(jnp.bfloat16)

                row_loop(rows, add)

        else:

            def add(at):
                half[i][at] = (
                    ins[i][core, at].astype(f32) + got[i][at].astype(f32)
                ).astype(jnp.bfloat16)

            row_loop(rows, add)
        for k in range(1, n):
            second[i, k] = remote(
                piece_of(i, lax.rem(me + k, n)),
                pieces[i].at[k - 1],
                b_send.at[i, k - 1],
                b_recv.at[i, k - 1],
                shard_peers[k - 1],
            )
            second[i, k].start()
    for i in range(count):
        for k in range(1, n):
            second[i, k].wait_recv()
        mine = piece_of(i, me)

        def add_pieces(at):
            total = mine[at].astype(f32)
            for k in range(1, n):
                total = total + pieces[i][k - 1, at].astype(f32)
            slots[i][chip, at] = total.astype(jnp.bfloat16)

        row_loop(outs[i].shape[1], add_pieces)
        for k in range(1, chips):
            third[i, k] = remote(
                slots[i].at[chip],
                slots[i].at[chip],
                c_send.at[i, k - 1],
                c_recv.at[i, k - 1],
                chip_peers[k - 1],
            )
            third[i, k].start()
    for i in range(count):
        for k in range(1, chips):
            third[i, k].wait_recv()

        def add_chips(at):
            total = slots[i][0, at].astype(f32)
            for q in range(1, chips):
                total = total + slots[i][q, at].astype(f32)
            outs[i][core, at] = total.astype(jnp.bfloat16)

        row_loop(outs[i].shape[1], add_chips)
        fourth.append(
            remote(outs[i].at[core], outs[i].at[core], d_send.at[i], d_recv.at[i], partner)
        )
        fourth[i].start()
    for copy in fourth:
        copy.wait()
    for copy in first + list(second.values()) + list(third.values()):
        copy.wait_send()


def sum_grads(grads, kinds, ident):
    n, m = lax.axis_size("shard"), lax.axis_size("replica")
    bf = jnp.bfloat16
    views, out, got, pieces, slots = [], [], [], [], []
    for g, kind in zip(grads, kinds):
        rows, cols = g.shape
        if kind == 0:
            deep, wide = rows // (2 * n), cols
            views.append(g.reshape(n, 2, deep, cols))
            got.append((n, deep, cols))
        else:
            deep, wide = rows // 2, cols // n
            views.append(g.reshape(2, deep, cols))
            got.append((deep, cols))
        out.append(jax.ShapeDtypeStruct((2, deep, wide), bf))
        pieces.append((max(n - 1, 1), deep, wide))
        slots.append((m // 2, deep, wide))
    count = len(grads)
    vmem = pl.BlockSpec(memory_space=pltpu.VMEM)
    one = pltpu.SemaphoreType.DMA((count,))
    by_shard = pltpu.SemaphoreType.DMA((count, max(n - 1, 1)))
    by_chip = pltpu.SemaphoreType.DMA((count, max(m // 2 - 1, 1)))
    total = sum(g.size * 2 for g in grads)
    res = pl.pallas_call(
        functools.partial(grad_kernel, n, m, kinds),
        out_shape=out,
        in_specs=[vmem] * count,
        out_specs=[vmem] * count,
        scratch_shapes=[pltpu.VMEM(t, bf) for t in got + got + pieces + slots]
        + [one, one, by_shard, by_shard, by_chip, by_chip, one, one],
        cost_estimate=pl.CostEstimate(
            flops=0, bytes_accessed=30 * total, transcendentals=0
        ),
        compiler_params=pltpu.CompilerParams(collective_id=ident, has_side_effects=True),
    )(*views)
    return [r.reshape(-1, r.shape[2]).astype(jnp.float32) for r in res]


def small_kernel(sizes, shared, local, out, *scratch):
    slots, send, recv = scratch[0:3], scratch[3:6], scratch[6:9]
    names = ("tensor", "replica", "shard")
    here = [lax.axis_index(name) for name in names]
    greet(
        [
            {names[a]: lax.rem(here[a] + k, sizes[a])}
            for a in range(3)
            for k in range(1, sizes[a])
        ]
    )
    deep = shared.shape[0]
    for a in range(3):
        if a == 0:
            slots[0][here[0]] = shared[...]
        copies = [
            remote(
                shared if a == 0 else slots[a].at[here[a]],
                slots[a].at[here[a]],
                send[a].at[k - 1],
                recv[a].at[k - 1],
                {names[a]: lax.rem(here[a] + k, sizes[a])},
            )
            for k in range(1, sizes[a])
        ]
        for copy in copies:
            copy.start()
        for copy in copies:
            copy.wait_recv()
        total = slots[a][0]
        for k in range(1, sizes[a]):
            total = total + slots[a][k]
        if a == 0:
            slots[1][here[1], 0:deep] = total
            slots[1][here[1], deep:] = local[...]
        elif a == 1:
            slots[2][here[2]] = total
        else:
            out[...] = total
        for copy in copies:
            copy.wait_send()


def as_rows(vec):
    flat = vec.reshape(-1)
    return jnp.pad(flat, (0, -flat.shape[0] % 1024)).reshape(-1, 128)


def sum_small(shared, local, ident):
    sizes = tuple(lax.axis_size(a) for a in ("tensor", "replica", "shard"))
    deep, low = shared.shape[0], local.shape[0]
    vmem = pl.BlockSpec(memory_space=pltpu.VMEM)
    sems = [pltpu.SemaphoreType.DMA((max(k - 1, 1),)) for k in sizes]
    return pl.pallas_call(
        functools.partial(small_kernel, sizes),
        out_shape=jax.ShapeDtypeStruct((deep + low, 128), jnp.float32),
        in_specs=[vmem] * 2,
        out_specs=vmem,
        scratch_shapes=[
            pltpu.VMEM((sizes[0], deep, 128), jnp.float32),
            pltpu.VMEM((sizes[1], deep + low, 128), jnp.float32),
            pltpu.VMEM((sizes[2], deep + low, 128), jnp.float32),
        ]
        + sems
        + sems,
        cost_estimate=pl.CostEstimate(flops=0, bytes_accessed=20000000, transcendentals=0),
        compiler_params=pltpu.CompilerParams(collective_id=ident, has_side_effects=True),
    )(shared, local)


def shards(
    block_in,
    segment_ids,
    grad_out,
    qkv_weight,
    qv_bias,
    out_weight,
    up_weight,
    up_bias,
    down_weight,
    norm_gains,
    shift_biases,
):
    small = (qv_bias, up_bias[None], norm_gains, shift_biases)
    inputs_bf = block_in.astype(jnp.bfloat16)
    input_rows_full = lax.all_gather(inputs_bf, "tensor", axis=1, tiled=True)
    cols = qkv_weight.shape[2]
    query_key_value_full, output_weight_full, packed = gather_blocks(
        (
            qkv_weight.reshape(-1, 3 * cols),
            out_weight,
            as_rows(
                jnp.concatenate([vec.reshape(-1) for vec in small]).astype(jnp.float32)
            ),
        ),
        (0, 1, 2),
        1,
    )
    packed = packed.reshape(packed.shape[0], -1)
    unpacked = []
    start = 0
    for vec in small:
        rows, piece = vec.shape
        part = packed[:, start : start + rows * piece].reshape(-1, rows, piece)
        unpacked.append(jnp.swapaxes(part, 0, 1).reshape(rows, -1))
        start += rows * piece
    qv_all, upbias_all, gain_all, shift_all = unpacked
    upbias_all = upbias_all[0]
    seqs = block_in.shape[0]
    width = block_in.shape[2]
    length = segment_ids.shape[1]
    heads_here = cols // HEAD_DIM
    scale = 1.0 / math.sqrt(HEAD_DIM)
    gain_full = gain_all.astype(jnp.float32)
    shift_full = shift_all.astype(jnp.float32)
    qv_full = qv_all.astype(jnp.float32)
    query_key_value = jnp.einsum(
        "agp,pm->agm", input_rows_full, query_key_value_full, preferred_element_type=jnp.float32
    )
    split = (seqs, length, heads_here, HEAD_DIM)
    query = (query_key_value[:, :, :cols] + qv_full[0]).astype(jnp.bfloat16).reshape(split)
    keys = query_key_value[:, :, cols : 2 * cols].astype(jnp.bfloat16).reshape(split)
    values = (query_key_value[:, :, 2 * cols :] + qv_full[1]).astype(jnp.bfloat16).reshape(split)
    same = (segment_ids[:, :, None] == segment_ids[:, None, :])[:, None]
    scores = jnp.einsum("sqhe,skhe->shqk", query, keys, preferred_element_type=jnp.float32) * scale
    scores = jnp.where(same, scores, masked_score)
    highest = jnp.max(scores, axis=-1, keepdims=True)
    expo = jnp.exp(scores - highest)
    total = jnp.sum(expo, axis=-1, keepdims=True)
    probs = (expo / total).astype(jnp.bfloat16)
    log_total = highest + jnp.log(total)
    attention_context = jnp.einsum(
        "shqk,skhe->sqhe", probs, values, preferred_element_type=jnp.float32
    )
    attention_context = attention_context.astype(jnp.bfloat16).reshape(seqs, length, cols)
    attention_slice = jnp.einsum(
        "nip,pr->nir", attention_context, output_weight_full, preferred_element_type=jnp.float32
    )
    up_weight, down_weight, attention_slice = lax.optimization_barrier(
        (up_weight, down_weight, attention_slice)
    )
    up_weight_full, down_weight_full = gather_blocks((up_weight, down_weight), (0, 1), 2)
    attended = scatter_sum(attention_slice, "tensor", 1).astype(jnp.float32)
    first_sum = block_in + (attended + shift_full[0])
    hidden, normed_one, inverse_one = norm_forward(first_sum, gain_full[0], shift_full[1])
    hidden_bf = hidden.astype(jnp.bfloat16)
    hidden_state_full = lax.all_gather(hidden_bf, "tensor", axis=1, tiled=True)
    pre_act = jnp.einsum(
        "peo,ot->pet", hidden_state_full, up_weight_full, preferred_element_type=jnp.float32
    ) + upbias_all.astype(jnp.float32)
    activ, slope = gelu_parts(pre_act)
    activation_bfloat = activ.astype(jnp.bfloat16)
    down_weight_slice = jnp.einsum(
        "uzt,tv->uzv", activation_bfloat, down_weight_full, preferred_element_type=jnp.float32
    )
    second_sum = hidden + (
        scatter_sum(down_weight_slice, "tensor", 1).astype(jnp.float32)
        + shift_full[2]
    )
    block_out, normed_two, inverse_two = norm_forward(second_sum, gain_full[1], shift_full[3])
    d_second = norm_backward(grad_out, normed_two, inverse_two, gain_full[1])
    second_gradient_full = lax.all_gather(
        d_second.astype(jnp.bfloat16), "tensor", axis=1, tiled=True
    )
    down_weight_gradient = jnp.einsum(
        "bct,bcm->tm", activation_bfloat, second_gradient_full, preferred_element_type=jnp.float32
    )
    d_pre = (
        jnp.einsum(
            "ajn,tn->ajt",
            second_gradient_full,
            down_weight_full,
            preferred_element_type=jnp.float32,
        )
        * slope
    )
    g_upbias = jnp.sum(d_pre, axis=(0, 1))
    preact_gradient_bfloat = d_pre.astype(jnp.bfloat16)
    up_weight_gradient = jnp.einsum(
        "ahk,ahp->kp", hidden_state_full, preact_gradient_bfloat, preferred_element_type=jnp.float32
    )
    hidden_state_slice = jnp.einsum(
        "ixj,gj->ixg", preact_gradient_bfloat, up_weight_full, preferred_element_type=jnp.float32
    )
    d_hidden = (
        scatter_sum(hidden_state_slice, "tensor", 1).astype(jnp.float32) + d_second
    )
    d_first = norm_backward(d_hidden, normed_one, inverse_one, gain_full[0])
    gain_part = jnp.stack(
        [jnp.sum(d_hidden * normed_one, axis=(0, 1)), jnp.sum(grad_out * normed_two, axis=(0, 1))]
    )
    shift_part = jnp.stack(
        [
            jnp.sum(d_first, axis=(0, 1)),
            jnp.sum(d_hidden, axis=(0, 1)),
            jnp.sum(d_second, axis=(0, 1)),
            jnp.sum(grad_out, axis=(0, 1)),
        ]
    )
    first_gradient_full = lax.all_gather(d_first.astype(jnp.bfloat16), "tensor", axis=1, tiled=True)
    output_weight_gradient = jnp.einsum(
        "unb,una->ba", attention_context, first_gradient_full, preferred_element_type=jnp.float32
    )
    context_gradient = jnp.einsum(
        "tbu,wu->tbw", first_gradient_full, output_weight_full, preferred_element_type=jnp.float32
    )
    context_gradient = context_gradient.astype(jnp.bfloat16).reshape(
        seqs, length, heads_here, HEAD_DIM
    )
    probs_back = jnp.exp(scores - log_total)
    d_probs = jnp.einsum(
        "sqhe,skhe->shqk", context_gradient, values, preferred_element_type=jnp.float32
    )
    row_dot = jnp.sum(probs_back * d_probs, axis=-1, keepdims=True)
    d_scores = (probs_back * (d_probs - row_dot)).astype(jnp.bfloat16)
    d_query = (
        jnp.einsum("shqk,skhe->sqhe", d_scores, keys, preferred_element_type=jnp.float32) * scale
    )
    d_keys = (
        jnp.einsum("shqk,sqhe->skhe", d_scores, query, preferred_element_type=jnp.float32) * scale
    )
    d_values = jnp.einsum(
        "shqk,sqhe->skhe",
        probs_back.astype(jnp.bfloat16),
        context_gradient,
        preferred_element_type=jnp.float32,
    )
    d_query = d_query.reshape(seqs, length, cols)
    d_keys = d_keys.reshape(seqs, length, cols)
    d_values = d_values.reshape(seqs, length, cols)
    g_qv = jnp.stack([jnp.sum(d_query, axis=(0, 1)), jnp.sum(d_values, axis=(0, 1))])
    projected_gradient_bfloat = jnp.concatenate([d_query, d_keys, d_values], axis=2).astype(jnp.bfloat16)
    projection_weight_gradient = jnp.einsum(
        "pjx,pjv->xv",
        input_rows_full,
        projected_gradient_bfloat,
        preferred_element_type=jnp.float32,
    )
    input_slice = jnp.einsum(
        "pxv,yv->pxy",
        projected_gradient_bfloat,
        query_key_value_full,
        preferred_element_type=jnp.float32,
    )
    grad_in = scatter_sum(input_slice, "tensor", 1).astype(jnp.float32) + d_first
    bf = jnp.bfloat16
    grad_up, grad_down = sum_grads(
        (up_weight_gradient.astype(bf), down_weight_gradient.astype(bf)), (0, 1), 3
    )
    grad_qkv_flat, grad_out_weight = sum_grads(
        (projection_weight_gradient.astype(bf), output_weight_gradient.astype(bf)), (0, 1), 4
    )
    grad_qkv = grad_qkv_flat.reshape(-1, 3, cols)
    shard_index = lax.axis_index("shard")
    shared = as_rows(jnp.concatenate([gain_part, shift_part]))
    sums = sum_small(shared, as_rows(jnp.concatenate([g_qv.reshape(-1), g_upbias])), 5)
    wide = sums[: shared.shape[0]].reshape(-1)[: 6 * width].reshape(6, width)
    gain_tot, shift_tot = wide[:2], wide[2:]
    own = sums[shared.shape[0] :].reshape(-1)
    qv_tot = own[: 2 * cols].reshape(2, cols)
    upbias_tot = own[2 * cols : 2 * cols + g_upbias.shape[0]]
    vec_piece = norm_gains.shape[1]
    qv_piece = qv_bias.shape[1]
    upbias_piece = up_bias.shape[0]
    grad_gains = lax.dynamic_slice_in_dim(gain_tot, shard_index * vec_piece, vec_piece, 1)
    grad_shifts = lax.dynamic_slice_in_dim(shift_tot, shard_index * vec_piece, vec_piece, 1)
    grad_qv = lax.dynamic_slice_in_dim(qv_tot, shard_index * qv_piece, qv_piece, 1)
    grad_upbias = lax.dynamic_slice_in_dim(upbias_tot, shard_index * upbias_piece, upbias_piece, 0)
    return (
        block_out,
        grad_in,
        grad_qkv,
        grad_qv,
        grad_out_weight,
        grad_up,
        grad_upbias,
        grad_down,
        grad_gains,
        grad_shifts,
    )


def solution(mesh):
    in_specs = (
        P(("shard", "replica"), "tensor", None),
        P(("shard", "replica"), None),
        P(("shard", "replica"), "tensor", None),
        P("shard", None, "tensor"),
        P(None, ("tensor", "shard")),
        P("tensor", "shard"),
        P("shard", "tensor"),
        P(("tensor", "shard")),
        P("tensor", "shard"),
        P(None, "shard"),
        P(None, "shard"),
    )
    out_specs = (
        P(("shard", "replica"), "tensor", None),
        P(("shard", "replica"), "tensor", None),
        P("shard", None, "tensor"),
        P(None, ("tensor", "shard")),
        P("tensor", "shard"),
        P("shard", "tensor"),
        P(("tensor", "shard")),
        P("tensor", "shard"),
        P(None, "shard"),
        P(None, "shard"),
    )
    return jax.shard_map(shards, mesh=mesh, in_specs=in_specs, out_specs=out_specs, check_vma=False)
```

```python
import functools
import math

import jax
import jax.numpy as jnp
from jax import lax
from jax.experimental import pallas as pl
from jax.experimental.pallas import tpu as pltpu
from jax.sharding import PartitionSpec as P

HEAD_DIM = 64


norm_eps = 1e-12
masked_score = -1e30


def norm_forward(summed, gain, shift):
    center = summed - jnp.mean(summed, axis=-1, keepdims=True)
    inverse = lax.rsqrt(jnp.mean(center * center, axis=-1, keepdims=True) + norm_eps)
    normed = center * inverse
    return (normed * gain + shift, normed, inverse)


def norm_backward(grad, normed, inverse, gain):
    scaled = grad * gain
    return inverse * (
        scaled
        - jnp.mean(scaled, axis=-1, keepdims=True)
        - normed * jnp.mean(scaled * normed, axis=-1, keepdims=True)
    )


def gelu_parts(pre_act):
    cumul = 0.5 * (1.0 + jax.scipy.special.erf(pre_act * 0.7071067811865476))
    density = jnp.exp(-0.5 * pre_act * pre_act) * 0.3989422804014327
    return (pre_act * cumul, cumul + pre_act * density)


def scatter_sum(part, axes, dim):
    return lax.psum_scatter(
        part.astype(jnp.bfloat16), axes, scatter_dimension=dim, tiled=True
    )


def remote(src, dst, send, recv, where):
    return pltpu.make_async_remote_copy(
        src_ref=src,
        dst_ref=dst,
        send_sem=send,
        recv_sem=recv,
        device_id=where,
        device_id_type=pl.DeviceIdType.MESH,
    )


def greet(peers):
    barrier = pltpu.get_barrier_semaphore()
    for where in peers:
        pl.semaphore_signal(
            barrier, inc=1, device_id=where, device_id_type=pl.DeviceIdType.MESH
        )
    pl.semaphore_wait(barrier, len(peers))


def block_of(ref, kind, shape, piece, half):
    rows, cols = shape
    depth = rows // 2
    if kind == 0:
        return ref.at[pl.ds(pl.multiple_of(piece * rows + half * depth, depth), depth), :]
    return ref.at[
        pl.ds(pl.multiple_of(half * depth, depth), depth),
        pl.ds(pl.multiple_of(piece * cols, cols), cols),
    ]


def gather_kernel(n, kinds, shapes, *refs):
    count = len(kinds)
    ins, outs = refs[:count], refs[count : 2 * count]
    local, far_send, far_recv, near_send, near_recv = refs[2 * count :]
    me = lax.axis_index("shard")
    rep = lax.axis_index("replica")
    core = lax.rem(rep, 2)
    partner = {"replica": rep + 1 - 2 * core}
    greet([{"shard": lax.rem(me + k, n)} for k in range(1, n)] + [partner])
    far, near = {}, {}
    for i in range(count):
        for k in range(1, n):
            where = {"shard": lax.rem(me + k, n)}
            if kinds[i] == 2:
                src, dst = ins[i], outs[i].at[me]
            else:
                depth = shapes[i][0] // 2
                src = ins[i].at[pl.ds(pl.multiple_of(core * depth, depth), depth), :]
                dst = block_of(outs[i], kinds[i], shapes[i], me, core)
            far[i, k] = remote(src, dst, far_send.at[i, k - 1], far_recv.at[i, k - 1], where)
            far[i, k].start()
    own = []
    for i in range(count):
        rows, cols = shapes[i]
        if kinds[i] == 2:
            dst = outs[i].at[me]
        elif kinds[i] == 0:
            dst = outs[i].at[pl.ds(pl.multiple_of(me * rows, rows), rows), :]
        else:
            dst = outs[i].at[:, pl.ds(pl.multiple_of(me * cols, cols), cols)]
        own.append(pltpu.make_async_copy(ins[i], dst, local.at[i]))
        own[-1].start()
    for i in range(count):
        for k in range(1, n):
            far[i, k].wait_recv()
            if kinds[i] != 2:
                block = block_of(outs[i], kinds[i], shapes[i], lax.rem(me + n - k, n), core)
                near[i, k] = remote(
                    block, block, near_send.at[i, k - 1], near_recv.at[i, k - 1], partner
                )
                near[i, k].start()
    for copy in near.values():
        copy.wait()
    for copy in far.values():
        copy.wait_send()
    for copy in own:
        copy.wait()


def gather_blocks(arrays, kinds, ident):
    n = lax.axis_size("shard")
    shapes = [a.shape for a in arrays]
    out = []
    for a, kind in zip(arrays, kinds):
        rows, cols = a.shape
        full = ((n * rows, cols), (rows, n * cols), (n, rows, cols))[kind]
        out.append(jax.ShapeDtypeStruct(full, a.dtype))
    vmem = pl.BlockSpec(memory_space=pltpu.VMEM)
    grid = (len(arrays), max(n - 1, 1))
    total = sum(a.size * a.dtype.itemsize for a in arrays) * n
    return pl.pallas_call(
        functools.partial(gather_kernel, n, kinds, shapes),
        out_shape=out,
        in_specs=[vmem] * len(arrays),
        out_specs=[vmem] * len(arrays),
        scratch_shapes=[pltpu.SemaphoreType.DMA((len(arrays),))]
        + [pltpu.SemaphoreType.DMA(grid)] * 4,
        cost_estimate=pl.CostEstimate(
            flops=0, bytes_accessed=20 * total, transcendentals=0
        ),
        compiler_params=pltpu.CompilerParams(collective_id=ident, has_side_effects=True),
    )(*arrays)


def row_loop(rows, body):
    step = min(rows, 32)

    @pl.loop(0, rows // step)
    def _(j):
        body(pl.ds(pl.multiple_of(j * step, step), step))


def grad_kernel(n, m, kinds, *refs):
    count = len(kinds)
    ins, outs = refs[:count], refs[count : 2 * count]
    got, half, pieces, slots = (refs[(2 + q) * count : (3 + q) * count] for q in range(4))
    a_send, a_recv, b_send, b_recv, c_send, c_recv, d_send, d_recv = refs[6 * count :]
    me = lax.axis_index("shard")
    rep = lax.axis_index("replica")
    core = lax.rem(rep, 2)
    chips = m // 2
    chip = rep // 2
    partner = {"replica": rep + 1 - 2 * core}
    shard_peers = [{"shard": lax.rem(me + k, n)} for k in range(1, n)]
    chip_peers = [{"replica": lax.rem(chip + k, chips) * 2 + core} for k in range(1, chips)]
    greet([partner] + shard_peers + chip_peers)
    f32 = jnp.float32
    first, second, third, fourth = [], {}, {}, []

    def piece_of(i, index):
        if kinds[i] == 0:
            return half[i].at[index]
        cols = outs[i].shape[2]
        return half[i].at[:, pl.ds(pl.multiple_of(index * cols, cols), cols)]

    for i in range(count):
        src = ins[i].at[:, 1 - core] if kinds[i] == 0 else ins[i].at[1 - core]
        first.append(remote(src, got[i], a_send.at[i], a_recv.at[i], partner))
        first[i].start()
    for i in range(count):
        first[i].wait_recv()
        rows = outs[i].shape[1]
        if kinds[i] == 0:

            @pl.loop(0, n)
            def _(p):
                def add(at):
                    half[i][p, at] = (
                        ins[i][p, core, at].astype(f32) + got[i][p, at].astype(f32)
                    ).astype(jnp.bfloat16)

                row_loop(rows, add)

        else:

            def add(at):
                half[i][at] = (
                    ins[i][core, at].astype(f32) + got[i][at].astype(f32)
                ).astype(jnp.bfloat16)

            row_loop(rows, add)
        for k in range(1, n):
            second[i, k] = remote(
                piece_of(i, lax.rem(me + k, n)),
                pieces[i].at[k - 1],
                b_send.at[i, k - 1],
                b_recv.at[i, k - 1],
                shard_peers[k - 1],
            )
            second[i, k].start()
    for i in range(count):
        for k in range(1, n):
            second[i, k].wait_recv()
        mine = piece_of(i, me)

        def add_pieces(at):
            total = mine[at].astype(f32)
            for k in range(1, n):
                total = total + pieces[i][k - 1, at].astype(f32)
            slots[i][chip, at] = total.astype(jnp.bfloat16)

        row_loop(outs[i].shape[1], add_pieces)
        for k in range(1, chips):
            third[i, k] = remote(
                slots[i].at[chip],
                slots[i].at[chip],
                c_send.at[i, k - 1],
                c_recv.at[i, k - 1],
                chip_peers[k - 1],
            )
            third[i, k].start()
    for i in range(count):
        for k in range(1, chips):
            third[i, k].wait_recv()

        def add_chips(at):
            total = slots[i][0, at].astype(f32)
            for q in range(1, chips):
                total = total + slots[i][q, at].astype(f32)
            outs[i][core, at] = total.astype(jnp.bfloat16)

        row_loop(outs[i].shape[1], add_chips)
        fourth.append(
            remote(outs[i].at[core], outs[i].at[core], d_send.at[i], d_recv.at[i], partner)
        )
        fourth[i].start()
    for copy in fourth:
        copy.wait()
    for copy in first + list(second.values()) + list(third.values()):
        copy.wait_send()


def sum_grads(grads, kinds, ident):
    n, m = lax.axis_size("shard"), lax.axis_size("replica")
    bf = jnp.bfloat16
    views, out, got, pieces, slots = [], [], [], [], []
    for g, kind in zip(grads, kinds):
        rows, cols = g.shape
        if kind == 0:
            deep, wide = rows // (2 * n), cols
            views.append(g.reshape(n, 2, deep, cols))
            got.append((n, deep, cols))
        else:
            deep, wide = rows // 2, cols // n
            views.append(g.reshape(2, deep, cols))
            got.append((deep, cols))
        out.append(jax.ShapeDtypeStruct((2, deep, wide), bf))
        pieces.append((max(n - 1, 1), deep, wide))
        slots.append((m // 2, deep, wide))
    count = len(grads)
    vmem = pl.BlockSpec(memory_space=pltpu.VMEM)
    one = pltpu.SemaphoreType.DMA((count,))
    by_shard = pltpu.SemaphoreType.DMA((count, max(n - 1, 1)))
    by_chip = pltpu.SemaphoreType.DMA((count, max(m // 2 - 1, 1)))
    total = sum(g.size * 2 for g in grads)
    res = pl.pallas_call(
        functools.partial(grad_kernel, n, m, kinds),
        out_shape=out,
        in_specs=[vmem] * count,
        out_specs=[vmem] * count,
        scratch_shapes=[pltpu.VMEM(t, bf) for t in got + got + pieces + slots]
        + [one, one, by_shard, by_shard, by_chip, by_chip, one, one],
        cost_estimate=pl.CostEstimate(
            flops=0, bytes_accessed=30 * total, transcendentals=0
        ),
        compiler_params=pltpu.CompilerParams(collective_id=ident, has_side_effects=True),
    )(*views)
    return [r.reshape(-1, r.shape[2]).astype(jnp.float32) for r in res]


def small_kernel(sizes, shared, local, out, *scratch):
    slots, send, recv = scratch[0:3], scratch[3:6], scratch[6:9]
    names = ("tensor", "replica", "shard")
    here = [lax.axis_index(name) for name in names]
    greet(
        [
            {names[a]: lax.rem(here[a] + k, sizes[a])}
            for a in range(3)
            for k in range(1, sizes[a])
        ]
    )
    deep = shared.shape[0]
    for a in range(3):
        if a == 0:
            slots[0][here[0]] = shared[...]
        copies = [
            remote(
                shared if a == 0 else slots[a].at[here[a]],
                slots[a].at[here[a]],
                send[a].at[k - 1],
                recv[a].at[k - 1],
                {names[a]: lax.rem(here[a] + k, sizes[a])},
            )
            for k in range(1, sizes[a])
        ]
        for copy in copies:
            copy.start()
        for copy in copies:
            copy.wait_recv()
        total = slots[a][0]
        for k in range(1, sizes[a]):
            total = total + slots[a][k]
        if a == 0:
            slots[1][here[1], 0:deep] = total
            slots[1][here[1], deep:] = local[...]
        elif a == 1:
            slots[2][here[2]] = total
        else:
            out[...] = total
        for copy in copies:
            copy.wait_send()


def as_rows(vec):
    flat = vec.reshape(-1)
    return jnp.pad(flat, (0, -flat.shape[0] % 1024)).reshape(-1, 128)


def sum_small(shared, local, ident):
    sizes = tuple(lax.axis_size(a) for a in ("tensor", "replica", "shard"))
    deep, low = shared.shape[0], local.shape[0]
    vmem = pl.BlockSpec(memory_space=pltpu.VMEM)
    sems = [pltpu.SemaphoreType.DMA((max(k - 1, 1),)) for k in sizes]
    return pl.pallas_call(
        functools.partial(small_kernel, sizes),
        out_shape=jax.ShapeDtypeStruct((deep + low, 128), jnp.float32),
        in_specs=[vmem] * 2,
        out_specs=vmem,
        scratch_shapes=[
            pltpu.VMEM((sizes[0], deep, 128), jnp.float32),
            pltpu.VMEM((sizes[1], deep + low, 128), jnp.float32),
            pltpu.VMEM((sizes[2], deep + low, 128), jnp.float32),
        ]
        + sems
        + sems,
        cost_estimate=pl.CostEstimate(flops=0, bytes_accessed=20000000, transcendentals=0),
        compiler_params=pltpu.CompilerParams(collective_id=ident, has_side_effects=True),
    )(shared, local)


def shards(
    block_in,
    segment_ids,
    grad_out,
    qkv_weight,
    qv_bias,
    out_weight,
    up_weight,
    up_bias,
    down_weight,
    norm_gains,
    shift_biases,
):
    small = (qv_bias, up_bias[None], norm_gains, shift_biases)
    inputs_bf = block_in.astype(jnp.bfloat16)
    input_rows_full = lax.all_gather(inputs_bf, "tensor", axis=1, tiled=True)
    cols = qkv_weight.shape[2]
    query_key_value_full, output_weight_full, packed = gather_blocks(
        (
            qkv_weight.reshape(-1, 3 * cols),
            out_weight,
            as_rows(
                jnp.concatenate([vec.reshape(-1) for vec in small]).astype(jnp.float32)
            ),
        ),
        (0, 1, 2),
        1,
    )
    packed = packed.reshape(packed.shape[0], -1)
    unpacked = []
    start = 0
    for vec in small:
        rows, piece = vec.shape
        part = packed[:, start : start + rows * piece].reshape(-1, rows, piece)
        unpacked.append(jnp.swapaxes(part, 0, 1).reshape(rows, -1))
        start += rows * piece
    qv_all, upbias_all, gain_all, shift_all = unpacked
    upbias_all = upbias_all[0]
    seqs = block_in.shape[0]
    width = block_in.shape[2]
    length = segment_ids.shape[1]
    heads_here = cols // HEAD_DIM
    scale = 1.0 / math.sqrt(HEAD_DIM)
    gain_full = gain_all.astype(jnp.float32)
    shift_full = shift_all.astype(jnp.float32)
    qv_full = qv_all.astype(jnp.float32)
    query_key_value = jnp.einsum(
        "agp,pm->agm", input_rows_full, query_key_value_full, preferred_element_type=jnp.float32
    )
    split = (seqs, length, heads_here, HEAD_DIM)
    query = (query_key_value[:, :, :cols] + qv_full[0]).astype(jnp.bfloat16).reshape(split)
    keys = query_key_value[:, :, cols : 2 * cols].astype(jnp.bfloat16).reshape(split)
    values = (query_key_value[:, :, 2 * cols :] + qv_full[1]).astype(jnp.bfloat16).reshape(split)
    same = (segment_ids[:, :, None] == segment_ids[:, None, :])[:, None]
    scores = jnp.einsum("sqhe,skhe->shqk", query, keys, preferred_element_type=jnp.float32) * scale
    scores = jnp.where(same, scores, masked_score)
    highest = jnp.max(scores, axis=-1, keepdims=True)
    expo = jnp.exp(scores - highest)
    total = jnp.sum(expo, axis=-1, keepdims=True)
    probs = (expo / total).astype(jnp.bfloat16)
    log_total = highest + jnp.log(total)
    attention_context = jnp.einsum(
        "shqk,skhe->sqhe", probs, values, preferred_element_type=jnp.float32
    )
    attention_context = attention_context.astype(jnp.bfloat16).reshape(seqs, length, cols)
    attention_slice = jnp.einsum(
        "nip,pr->nir", attention_context, output_weight_full, preferred_element_type=jnp.float32
    )
    up_weight, down_weight, attention_slice = lax.optimization_barrier(
        (up_weight, down_weight, attention_slice)
    )
    up_weight_full, down_weight_full = gather_blocks((up_weight, down_weight), (0, 1), 2)
    attended = scatter_sum(attention_slice, "tensor", 1).astype(jnp.float32)
    first_sum = block_in + (attended + shift_full[0])
    hidden, normed_one, inverse_one = norm_forward(first_sum, gain_full[0], shift_full[1])
    hidden_bf = hidden.astype(jnp.bfloat16)
    hidden_state_full = lax.all_gather(hidden_bf, "tensor", axis=1, tiled=True)
    pre_act = jnp.einsum(
        "peo,ot->pet", hidden_state_full, up_weight_full, preferred_element_type=jnp.float32
    ) + upbias_all.astype(jnp.float32)
    activ, slope = gelu_parts(pre_act)
    activation_bfloat = activ.astype(jnp.bfloat16)
    down_weight_slice = jnp.einsum(
        "uzt,tv->uzv", activation_bfloat, down_weight_full, preferred_element_type=jnp.float32
    )
    second_sum = hidden + (
        scatter_sum(down_weight_slice, "tensor", 1).astype(jnp.float32)
        + shift_full[2]
    )
    block_out, normed_two, inverse_two = norm_forward(second_sum, gain_full[1], shift_full[3])
    d_second = norm_backward(grad_out, normed_two, inverse_two, gain_full[1])
    second_gradient_full = lax.all_gather(
        d_second.astype(jnp.bfloat16), "tensor", axis=1, tiled=True
    )
    d_pre = (
        jnp.einsum(
            "ajn,tn->ajt",
            second_gradient_full,
            down_weight_full,
            preferred_element_type=jnp.float32,
        )
        * slope
    )
    g_upbias = jnp.sum(d_pre, axis=(0, 1))
    preact_gradient_bfloat = d_pre.astype(jnp.bfloat16)
    up_weight_gradient = jnp.einsum(
        "ahk,ahp->kp", hidden_state_full, preact_gradient_bfloat, preferred_element_type=jnp.float32
    )
    hidden_state_slice = jnp.einsum(
        "ixj,gj->ixg", preact_gradient_bfloat, up_weight_full, preferred_element_type=jnp.float32
    )
    bf = jnp.bfloat16
    hidden_state_slice, activation_late = lax.optimization_barrier(
        (hidden_state_slice.astype(bf), activation_bfloat)
    )
    down_weight_gradient = jnp.einsum(
        "bct,bcm->tm", activation_late, second_gradient_full, preferred_element_type=jnp.float32
    )
    (grad_down,) = sum_grads((down_weight_gradient.astype(bf),), (1,), 3)
    hidden_scattered, grad_down = lax.optimization_barrier(
        (scatter_sum(hidden_state_slice, "tensor", 1), grad_down)
    )
    d_hidden = hidden_scattered.astype(jnp.float32) + d_second
    d_first = norm_backward(d_hidden, normed_one, inverse_one, gain_full[0])
    gain_part = jnp.stack(
        [jnp.sum(d_hidden * normed_one, axis=(0, 1)), jnp.sum(grad_out * normed_two, axis=(0, 1))]
    )
    shift_part = jnp.stack(
        [
            jnp.sum(d_first, axis=(0, 1)),
            jnp.sum(d_hidden, axis=(0, 1)),
            jnp.sum(d_second, axis=(0, 1)),
            jnp.sum(grad_out, axis=(0, 1)),
        ]
    )
    d_first_bf, up_weight_gradient = lax.optimization_barrier(
        (d_first.astype(bf), up_weight_gradient.astype(bf))
    )
    (grad_up,) = sum_grads((up_weight_gradient,), (0,), 4)
    first_gradient_full, grad_up = lax.optimization_barrier(
        (lax.all_gather(d_first_bf, "tensor", axis=1, tiled=True), grad_up)
    )
    output_weight_gradient = jnp.einsum(
        "unb,una->ba", attention_context, first_gradient_full, preferred_element_type=jnp.float32
    )
    context_gradient = jnp.einsum(
        "tbu,wu->tbw", first_gradient_full, output_weight_full, preferred_element_type=jnp.float32
    )
    context_gradient = context_gradient.astype(jnp.bfloat16).reshape(
        seqs, length, heads_here, HEAD_DIM
    )
    probs_back = jnp.exp(scores - log_total)
    d_probs = jnp.einsum(
        "sqhe,skhe->shqk", context_gradient, values, preferred_element_type=jnp.float32
    )
    row_dot = jnp.sum(probs_back * d_probs, axis=-1, keepdims=True)
    d_scores = (probs_back * (d_probs - row_dot)).astype(jnp.bfloat16)
    d_query = (
        jnp.einsum("shqk,skhe->sqhe", d_scores, keys, preferred_element_type=jnp.float32) * scale
    )
    d_keys = (
        jnp.einsum("shqk,sqhe->skhe", d_scores, query, preferred_element_type=jnp.float32) * scale
    )
    d_values = jnp.einsum(
        "shqk,sqhe->skhe",
        probs_back.astype(jnp.bfloat16),
        context_gradient,
        preferred_element_type=jnp.float32,
    )
    d_query = d_query.reshape(seqs, length, cols)
    d_keys = d_keys.reshape(seqs, length, cols)
    d_values = d_values.reshape(seqs, length, cols)
    g_qv = jnp.stack([jnp.sum(d_query, axis=(0, 1)), jnp.sum(d_values, axis=(0, 1))])
    projected_gradient_bfloat = jnp.concatenate([d_query, d_keys, d_values], axis=2).astype(jnp.bfloat16)
    projection_parts = [
        jnp.einsum(
            "pjx,pjv->xv", input_rows_full, part.astype(bf), preferred_element_type=jnp.float32
        )
        for part in (d_query, d_keys, d_values)
    ]
    input_slice = jnp.einsum(
        "pxv,yv->pxy",
        projected_gradient_bfloat,
        query_key_value_full,
        preferred_element_type=jnp.float32,
    )
    grad_in = scatter_sum(input_slice, "tensor", 1).astype(jnp.float32) + d_first
    grad_q, grad_k, grad_v, grad_out_weight = sum_grads(
        tuple(part.astype(bf) for part in projection_parts)
        + (output_weight_gradient.astype(bf),),
        (0, 0, 0, 1),
        5,
    )
    grad_qkv = jnp.stack([grad_q, grad_k, grad_v], axis=1)
    shard_index = lax.axis_index("shard")
    shared = as_rows(jnp.concatenate([gain_part, shift_part]))
    sums = sum_small(shared, as_rows(jnp.concatenate([g_qv.reshape(-1), g_upbias])), 6)
    wide = sums[: shared.shape[0]].reshape(-1)[: 6 * width].reshape(6, width)
    gain_tot, shift_tot = wide[:2], wide[2:]
    own = sums[shared.shape[0] :].reshape(-1)
    qv_tot = own[: 2 * cols].reshape(2, cols)
    upbias_tot = own[2 * cols : 2 * cols + g_upbias.shape[0]]
    vec_piece = norm_gains.shape[1]
    qv_piece = qv_bias.shape[1]
    upbias_piece = up_bias.shape[0]
    grad_gains = lax.dynamic_slice_in_dim(gain_tot, shard_index * vec_piece, vec_piece, 1)
    grad_shifts = lax.dynamic_slice_in_dim(shift_tot, shard_index * vec_piece, vec_piece, 1)
    grad_qv = lax.dynamic_slice_in_dim(qv_tot, shard_index * qv_piece, qv_piece, 1)
    grad_upbias = lax.dynamic_slice_in_dim(upbias_tot, shard_index * upbias_piece, upbias_piece, 0)
    return (
        block_out,
        grad_in,
        grad_qkv,
        grad_qv,
        grad_out_weight,
        grad_up,
        grad_upbias,
        grad_down,
        grad_gains,
        grad_shifts,
    )


def solution(mesh):
    in_specs = (
        P(("shard", "replica"), "tensor", None),
        P(("shard", "replica"), None),
        P(("shard", "replica"), "tensor", None),
        P("shard", None, "tensor"),
        P(None, ("tensor", "shard")),
        P("tensor", "shard"),
        P("shard", "tensor"),
        P(("tensor", "shard")),
        P("tensor", "shard"),
        P(None, "shard"),
        P(None, "shard"),
    )
    out_specs = (
        P(("shard", "replica"), "tensor", None),
        P(("shard", "replica"), "tensor", None),
        P("shard", None, "tensor"),
        P(None, ("tensor", "shard")),
        P("tensor", "shard"),
        P("shard", "tensor"),
        P(("tensor", "shard")),
        P("tensor", "shard"),
        P(None, "shard"),
        P(None, "shard"),
    )
    return jax.shard_map(shards, mesh=mesh, in_specs=in_specs, out_specs=out_specs, check_vma=False)
```
